32 devices in a mesh: groups: 2 (over x), blk: 4 (over y, core), rows: 4 (over z).
Axes of the slice: x: 2, y: 2, z: 4, core: 2. Of those that a mesh axis runs over, the one named last changes fastest.
Arguments:
- frame_one: float32 [4096, 256], P(('groups', 'blk', 'rows')), parts along dimension 0, may hold values from -6 to 6
- frame_two: float32 [4096, 256], P(('groups', 'blk', 'rows')), parts along dimension 0, may hold values from -6 to 6
- cot_zero: float32 [4096, 2048], P(('groups', 'blk', 'rows')), parts along dimension 0, may hold values from -0.375 to 0.375
- cot_one: float32 [4096, 512], P(('groups', 'blk', 'rows')), parts along dimension 0, may hold values from -1.5 to 1.5
- cot_two: float32 [4096, 128], P(('groups', 'blk', 'rows')), parts along dimension 0, may hold values from -6 to 6
- cot_three: float32 [4096, 32], P(('groups', 'blk', 'rows')), parts along dimension 0, may hold values from -24 to 24
Outputs:
- corr_zero: float32 [4096, 2048], P(('groups', 'blk', 'rows')), parts along dimension 0
- corr_one: float32 [4096, 512], P(('groups', 'blk', 'rows')), parts along dimension 0
- corr_two: float32 [4096, 128], P(('groups', 'blk', 'rows')), parts along dimension 0
- corr_three: float32 [4096, 32], P(('groups', 'blk', 'rows')), parts along dimension 0
- grad_one: float32 [256, 4096], P('rows', ('groups', 'blk')), parts along dimension 1
- grad_two: float32 [256, 4096], P('rows', ('groups', 'blk')), parts along dimension 1
The draws below stay inside these ranges and needn't reach their ends.
There are 2 independent parts, one for each index of `groups`. The reference program is written for one: setup_inputs(seed, part) draws one part's arguments, and reference() takes and returns one part's arrays. A program takes and returns all parts, laid end to end along the dimension named above; each array names one. Nothing has to cross between parts.
All inputs are finite; a program needn't handle non-finite values.
Results may differ from the reference program's by a relative error of at most 0.0001.
Values sent between devices are 32-bit elements; how exact they have to be, the bound alone decides.
A program may use at most 64 MiB of HBM per device.

```python
import math
import jax
import jax.numpy as jnp
from jax import lax

C = 256
LEVELS = 4
TROWS = 8
W2 = 64
BAND = 128
P2 = 2048
P1 = 2048
N_BLK = 4
N_ROWS = 4


def levels(own_key, shape, pieces, least, high):
    factor_of = 1.0
    for position, parts in pieces:
        draws = jax.random.uniform(jax.random.fold_in(jax.random.fold_in(own_key, 6), position), (parts,), jnp.float32, least / len(pieces), high / len(pieces))
        factor_of = factor_of * jnp.repeat(jnp.exp(draws), shape[position] // parts).reshape((-1,) + (1,) * (len(shape) - 1 - position))
    return factor_of


def normal_values(key, extent, width, most, shards=(), held_as=jnp.bfloat16):
    loudness = levels(key, extent, shards, -0.22, 0.18) if shards else 1.0
    values = jax.random.normal(key, extent, jnp.float32) * width * loudness
    return jnp.minimum(jnp.maximum(values, -most), most).astype(held_as)


def setup_inputs(seed: int = 0, part: int = 0) -> dict:
    splits = jax.random.split(jax.random.key(seed), 7)
    own_keys = jax.random.split(jax.random.fold_in(splits[6], part), 7)
    return {
        "frame_one": normal_values(own_keys[0], (P1, C), 1.0, 6.0, ((0, 16),), jnp.float32),
        "frame_two": normal_values(own_keys[1], (P2, C), 1.0, 6.0, ((0, 16),), jnp.float32),
        "cot_zero": normal_values(own_keys[2], (P1, P2), 0.0625, 0.375, ((0, 16),), jnp.float32),
        "cot_one": normal_values(own_keys[3], (P1, P2 // 4), 0.25, 1.5, ((0, 16),), jnp.float32),
        "cot_two": normal_values(own_keys[4], (P1, P2 // 16), 1.0, 6.0, ((0, 16),), jnp.float32),
        "cot_three": normal_values(own_keys[5], (P1, P2 // 64), 4.0, 24.0, ((0, 16),), jnp.float32),
    }


highest = lax.Precision.HIGHEST

def pool_once(volume, rows_now, cols_now):
    count_rows = volume.shape[0]
    shaped = volume.reshape(count_rows, rows_now // 2, 2, cols_now // 2, 2)
    return lax.optimization_barrier(jnp.mean(shaped, axis=(2, 4))).reshape(count_rows, rows_now // 2 * (cols_now // 2))

def spread_up(coarse, rows_now, cols_now):
    count_rows = coarse.shape[0]
    shaped = coarse.reshape(count_rows, rows_now, 1, cols_now, 1)
    widened = jnp.broadcast_to(shaped, (count_rows, rows_now, 2, cols_now, 2))
    return widened.reshape(count_rows, 4 * rows_now * cols_now) * 0.25

def reference(frame_one, frame_two, cot_zero, cot_one, cot_two, cot_three):
    inv_root = 1.0 / math.sqrt(C)
    image_rows = TROWS * N_BLK
    block_rows = BAND * N_ROWS
    cots = (cot_zero, cot_one, cot_two, cot_three)
    shaped_one = frame_one.reshape(N_BLK, block_rows, C)
    shaped_cots = tuple((cot.reshape(N_BLK, block_rows, cot.shape[1]) for cot in cots))

    def block_step(grad_accum, inputs):
        rows_blk = inputs[0]
        block_cots = inputs[1:]
        volume = jnp.dot(rows_blk, frame_two.T, precision=highest, preferred_element_type=jnp.float32) * inv_root
        levels_out = [volume]
        rows_now = image_rows
        cols_now = W2
        for level_idx in range(LEVELS - 1):
            volume = pool_once(volume, rows_now, cols_now)
            rows_now = rows_now // 2
            cols_now = cols_now // 2
            levels_out.append(volume)
        cot_total = block_cots[LEVELS - 1]
        for level_idx in range(LEVELS - 2, -1, -1):
            cot_total = block_cots[level_idx] + spread_up(cot_total, rows_now, cols_now)
            rows_now = rows_now * 2
            cols_now = cols_now * 2
        scaled = cot_total * inv_root
        grad_rows = jnp.dot(scaled, frame_two, precision=highest, preferred_element_type=jnp.float32)
        grad_accum = grad_accum + jnp.dot(scaled.T, rows_blk, precision=highest, preferred_element_type=jnp.float32)
        return (grad_accum, tuple(levels_out) + (grad_rows,))
    start_accum = jnp.zeros((P2, C), jnp.float32)
    grad_accum, outputs = lax.scan(block_step, start_accum, (shaped_one,) + shaped_cots)
    corr_zero = outputs[0].reshape(P1, P2)
    corr_one = outputs[1].reshape(P1, P2 // 4)
    corr_two = outputs[2].reshape(P1, P2 // 16)
    corr_three = outputs[3].reshape(P1, P2 // 64)
    grad_one = outputs[4].reshape(P1, C).T
    grad_two = grad_accum.T
    return (corr_zero, corr_one, corr_two, corr_three, grad_one, grad_two)
```

```python
import functools
import math

import jax
import jax.numpy as jnp
from jax import lax
from jax.experimental import pallas as pl
from jax.experimental.pallas import tpu as pltpu
from jax.sharding import PartitionSpec as P

TROWS = 8
W2 = 64
CORES = 2
TILE = TROWS * W2
POOL1 = TILE // 4
POOL2 = TILE // 16
POOL3 = TILE // 64
POOLED = 2 * POOL1
CUTS = 2
BITS = 4

f32 = jnp.float32
bf16 = jnp.bfloat16


def split(x):
    high = x.astype(bf16)
    low = (x - high.astype(f32)).astype(bf16)
    return high, low


def mm(a, b, ca, cb):
    return lax.dot_general(a, b, (((ca,), (cb,)), ((), ())), preferred_element_type=f32)


def pool_table():
    shape = (TILE, POOLED)
    pixel = lax.broadcasted_iota(jnp.int32, (TILE, 1), 0)
    row, col = pixel // W2, pixel % W2
    one = lax.shift_right_logical(row, 1) * (W2 // 2) + lax.shift_right_logical(col, 1)
    two = lax.shift_right_logical(row, 2) * (W2 // 4) + lax.shift_right_logical(col, 2) + POOL1
    three = lax.shift_right_logical(row, 3) * (W2 // 8) + lax.shift_right_logical(col, 3) + (
        POOL1 + POOL2)
    slot = lax.broadcasted_iota(jnp.int32, shape, 1)
    value = jnp.where(slot == one, 0.25, 0.0)
    value = jnp.where(slot == two, 0.0625, value)
    value = jnp.where(slot == three, 0.015625, value)
    return value.astype(bf16)


def kernel(tiles, rows_n, f1_in, f2_in, c0_in, c1_in, c2_in, c3_in,
           o0, o1, o2, o3, g1_out, g2_out,
           f1, f2, c0, c1, c2, c3t, coarse, scaled, table, f1s, f1t, acc, cin, yin, pin, qin, zin,
           pooled, gacc, g1t,
           in_sem, ag_recv, own_send, ys_send, cs_send, zf_send, nf_send, mf_send,
           rc_send, rc_recv, ry_send, ry_recv, rp_send, rp_recv, rq_send, rq_recv, rz_send, rz_recv,
           g_send, g_recv):
    band = f1.shape[0]
    chans = f1.shape[1]
    band2 = f2_in.shape[0]
    ys_n = tiles // CORES
    inv_root = 1.0 / math.sqrt(chans)
    blk = lax.axis_index("blk")
    z = lax.axis_index("rows")
    core = blk % CORES
    y = blk // CORES
    other = 1 - core
    sib = {"blk": y * CORES + other}

    def at_z(k):
        zz, bit = z, 1
        while bit < rows_n:
            if k % (2 * bit) >= bit:
                zz = zz + bit - 2 * bit * (z // bit % 2)
            bit *= 2
        return zz

    def at_y(k):
        return (y + k) % ys_n

    def y_peer(k):
        return {"blk": at_y(k) * CORES + core}

    partner = at_z(1)
    inner = (z + z // 2) % 2 == 1
    outer = (z + z // 2) % 2 == 0
    pairs = range(2, rows_n, 2)

    def far_inner(k):
        pair = at_z(k) // 2
        return pair * 2 + 1 - pair % 2

    def far_outer(k):
        pair = at_z(k) // 2
        return pair * 2 + pair % 2

    def span(t, zz):
        return pl.ds(pl.multiple_of(t * TILE + zz * band2, 8), band2)

    def piece(t, zz, h):
        rows = band2 // BITS
        return pl.ds(pl.multiple_of(t * TILE + zz * band2 + h * rows, 8), rows)

    loads = {}
    for i, (name, src, dst) in enumerate((
            ("f1", f1_in, f1), ("f2", f2_in, f2.at[span(blk, z), :]), ("c3", c3_in, c3t),
            ("c2", c2_in, c2), ("c1", c1_in, c1), ("c0", c0_in, c0))):
        loads[name] = pltpu.make_async_copy(src, dst, in_sem.at[i])
        loads[name].start()

    peers = [{"rows": at_z(k)} for k in range(1, rows_n)]
    peers += [y_peer(k) for k in range(1, ys_n)]
    peers += [sib]
    barrier = pltpu.get_barrier_semaphore()
    for peer in peers:
        pl.semaphore_signal(barrier, inc=1, device_id=peer)
    table[...] = pool_table()
    loads["f1"].wait()
    high, low = split(f1[...])
    f1s[0:band, :] = high
    f1s[band:, :] = low
    turned = f1[...].T
    high, low = split(turned)
    f1t[:, 0:band] = high
    f1t[:, band:] = low
    loads["c3"].wait()
    loads["c2"].wait()
    loads["c1"].wait()
    c3 = c3t[...].T
    for t in range(tiles):
        coarse[t] = jnp.concatenate(
            [c1[:, t * POOL1:(t + 1) * POOL1], c2[:, t * POOL2:(t + 1) * POOL2],
             c3[:, t * POOL3:(t + 1) * POOL3],
             jnp.zeros((band, POOLED - POOL1 - POOL2 - POOL3), f32)], axis=1)
    loads["f2"].wait()
    pl.semaphore_wait(barrier, len(peers))

    sent = []

    def await_(ref, rsem):
        pltpu.make_async_copy(ref, ref, rsem).wait()

    role = None

    def send(make):
        def copy():
            src, dst, ssem, rsem, peer = make()
            return pltpu.make_async_remote_copy(
                src_ref=src, dst_ref=dst, send_sem=ssem, recv_sem=rsem,
                device_id=peer, device_id_type=pl.DeviceIdType.MESH)

        copy().start()
        sent.append((copy, role))

    def drain(some):
        for copy, when in some:
            if when is None:
                copy().wait_send()
        for when in (inner, outer):
            @pl.when(when)
            def _():
                for copy, mine in some:
                    if mine is when:
                        copy().wait_send()

    def whole_wait(t, zz):
        await_(f2.at[span(t, zz), :], ag_recv.at[t * rows_n + zz, 0])

    def piece_wait(t, zz, h):
        await_(f2.at[piece(t, zz, h), :], ag_recv.at[t * rows_n + zz, h])

    def whole(t, zz, ssem, peer, src=None):
        where = f2.at[span(t, zz), :]
        return where if src is None else src, where, ssem, ag_recv.at[t * rows_n + zz, 0], peer

    def cut(t, zz, h, ssem, peer, src=None):
        where = f2.at[piece(t, zz, h), :]
        return where if src is None else src, where, ssem, ag_recv.at[t * rows_n + zz, h], peer

    def to_sib(t, zz, src=None):
        send(lambda: whole(t(), zz(), cs_send.at[t() * rows_n + zz()], sib, src))

    def own_tile():
        return blk

    def y_tile(k):
        return lambda: at_y(k) * CORES + core

    def here():
        return z

    def beside():
        return partner

    ks = list(range(1, ys_n))
    ends = (far_inner, far_outer)
    for k in ks:
        send(lambda k=k: whole(blk, z, ys_send.at[k - 1, z, 0], y_peer(k)))
    for h in range(BITS):
        send(lambda h=h: cut(blk, z, h, own_send.at[0, h], {"rows": partner}))
    role = inner

    @pl.when(inner)
    def _():
        for h in range(BITS):
            for j in pairs:
                send(lambda j=j, h=h: cut(blk, z, h, own_send.at[j // 2, h],
                                          {"rows": far_inner(j)}))

    role = None
    to_sib(own_tile, here)

    loads["c0"].wait()

    def band_sum(t):
        high, low = split(coarse[t])
        spread = mm(jnp.concatenate([high, low], axis=0), table[...], 1, 1)
        total = c0[:, pl.ds(pl.multiple_of(t * TILE, TILE), TILE)] + (spread[:band] + spread[band:])
        high, low = split(total * inv_root)
        scaled[t, 0:band, :] = high
        scaled[t, band:, :] = low
        twice = jnp.concatenate([high, high], axis=0)
        value = mm(f1t[...], twice, 1, 0) + mm(f1t[:, 0:band], low, 1, 0)
        acc[t] = value.reshape(acc.shape[1:])

    def to_chip(k):
        yy = at_y(k)
        band_sum(yy * CORES + other)
        send(lambda: (acc.at[at_y(k) * CORES + other], cin.at[at_y(k)], rc_send.at[at_y(k)],
                      rc_recv.at[at_y(k)], sib))

    def chip_sum(k):
        yy = at_y(k)
        await_(cin.at[yy], rc_recv.at[yy])
        acc[yy * CORES + core] += cin[yy]

    def sums_to_y(k, zz):
        for h in range(CUTS):
            send(lambda h=h: (
                acc.at[y_tile(k)(), zz(), h], yin.at[k - 1, zz(), h],
                ry_send.at[k - 1, zz(), h], ry_recv.at[k - 1, zz(), h], y_peer(k)))

    def add_y(zz, h):
        for k in ks:
            await_(yin.at[k - 1, zz, h], ry_recv.at[k - 1, zz, h])
            acc[blk, zz, h] += yin[k - 1, zz, h]

    def far(j, w):
        return lambda: ends[w](j)

    for k in ks:
        to_chip(k)
    to_chip(0)
    for k in ks:
        band_sum(y_tile(k)())
        chip_sum(k)
        for j in pairs:
            for w in range(2):
                sums_to_y(k, far(j, w))
    band_sum(blk)

    wide = 2 * band2
    started = []

    def work(t, name, pair):
        at = pl.multiple_of(t * TILE + pair * wide, wide)
        part = pl.ds(pl.multiple_of(pair * wide, wide), wide)
        high, low = split(f2[pl.ds(at, wide), :])
        both = mm(f1s[...], high, 1, 1)
        value = (both[:band] + both[band:] + mm(f1s[0:band, :], low, 1, 1)) * inv_root
        o0[:, pl.ds(at, wide)] = value
        vh, vl = split(value)
        both = mm(jnp.concatenate([vh, vl], axis=0), table[part, :], 1, 0)
        both = both[:band] + both[band:]
        ones = pl.ds(pl.multiple_of(t * POOL1, POOL1), POOL1)
        if name in started:
            pooled[t] += both[:, POOL1:]
            o1[:, ones] += both[:, :POOL1]
        else:
            pooled[t] = both[:, POOL1:]
            o1[:, ones] = both[:, :POOL1]
        both = mm(scaled[t, :, part], high, 1, 0)
        grad = both[:band] + both[band:] + mm(scaled[t, 0:band, part], low, 1, 0)
        if started:
            gacc[...] += grad
        else:
            gacc[...] = grad
        started.append(name)

    def near_work(t, name):
        work(t, name, z // 2)

    def far_work(t, name):
        for j in pairs:
            work(t, name, at_z(j) // 2)

    def forward(j, w, h, peers, on):
        piece_wait(blk, ends[w](j), h)
        if on:
            send(lambda: cut(blk, ends[w](j), h, nf_send.at[j - 2 + w, h], {"rows": partner}))
        for k in peers:
            send(lambda k=k: cut(blk, ends[w](j), h, ys_send.at[k - 1, ends[w](j), h], y_peer(k)))
        if h == BITS - 1:
            to_sib(own_tile, far(j, w))

    def partner_piece(h, on):
        piece_wait(blk, partner, h)
        if on:
            for j in pairs:
                send(lambda j=j: cut(blk, partner, h, mf_send.at[0, j // 2 - 1, h],
                                     {"rows": far_inner(j)}))
        if h == BITS - 1:
            to_sib(own_tile, beside)

    def y_shard(k, on):
        whole_wait(y_tile(k)(), z)
        if on:
            for h in range(BITS):
                for j in pairs:
                    send(lambda j=j, h=h: cut(y_tile(k)(), z, h, mf_send.at[k, j // 2 - 1, h],
                                              {"rows": far_inner(j)}))
        to_sib(y_tile(k), here)

    def turn(k):
        send(lambda: whole(y_tile(k)(), z, zf_send.at[k - 1], {"rows": partner}))

    def sums(j, w, h, on):
        add_y(ends[w](j), h)
        if on:
            send(lambda: (acc.at[blk, ends[w](j), h], pin.at[j - 2 + w, h],
                          rp_send.at[j - 2 + w, h], rp_recv.at[j - 2 + w, h],
                          {"rows": partner}))

    def combine(j, w, h):
        await_(pin.at[j - 2 + w, h], rp_recv.at[j - 2 + w, h])
        acc[blk, ends[w](j), h] += pin[j - 2 + w, h]
        send(lambda: (acc.at[blk, ends[w](j), h], zin.at[j // 2, h],
                      rz_send.at[j - 1 + w, h], rz_recv.at[j // 2, h],
                      {"rows": ends[w](j)}))

    def partner_sums(h):
        send(lambda: (acc.at[blk, partner, h], zin.at[0, h], rz_send.at[0, h], rz_recv.at[0, h],
                      {"rows": partner}))

    def sib_wait():
        for zz in range(rows_n):
            whole_wait(y * CORES + other, zz)

    bits = [[(j, w, h) for j in pairs for h in range(BITS)] for w in range(2)]
    halves = [(j, w, h) for j in pairs for w in range(2) for h in range(CUTS)]
    inners = [(j, w, h) for j, w, h in halves if w == 0]
    outers = [(j, w, h) for j, w, h in halves if w == 1]

    role = inner

    @pl.when(inner)
    def _():
        for k in ks:
            sums_to_y(k, beside)
        partner_piece(0, True)
        for j, w, h in bits[0]:
            if h and j == 2:
                partner_piece(h, True)
            forward(j, w, h, [], True)
        for k in ks:
            y_shard(k, True)
        for j, w, h in bits[1]:
            forward(j, w, h, ks, True)
        for k in ks:
            turn(k)
        for k in ks:
            for h in range(CUTS):
                await_(qin.at[k - 1, h], rq_recv.at[k - 1, h])
                acc[y_tile(k)(), z, h] += qin[k - 1, h]
            sums_to_y(k, here)
        chip_sum(0)
        for j, w, h in inners:
            sums(j, w, h, False)
        near_work(blk, "own")
        for j, w, h in outers:
            sums(j, w, h, False)
        far_work(blk, "own")
        for j, w, h in inners:
            combine(j, w, h)
        for h in range(CUTS):
            add_y(partner, h)
            partner_sums(h)
        sib_wait()
        near_work(y * CORES + other, "sib")
        far_work(y * CORES + other, "sib")
        for j, w, h in outers:
            combine(j, w, h)

    started.clear()
    role = outer

    @pl.when(outer)
    def _():
        for k in ks:
            for h in range(CUTS):
                send(lambda k=k, h=h: (
                    acc.at[y_tile(k)(), partner, h], qin.at[k - 1, h], rq_send.at[k - 1, h],
                    rq_recv.at[k - 1, h], {"rows": partner}))
        for h in range(BITS):
            partner_piece(h, False)
        for k in ks:
            y_shard(k, False)
        chip_sum(0)
        step = BITS // CUTS
        for i, (j, w, h) in enumerate(halves):
            sums(j, w, h, True)
            for b in range(h * step, h * step + step):
                forward(j, w, b, ks, False)
            if i == 1:
                for k in ks:
                    turn(k)
        for k in ks:
            sums_to_y(k, here)
        for h in range(CUTS):
            partner_sums(h)
        near_work(blk, "own")
        far_work(blk, "own")
        sib_wait()
        near_work(y * CORES + other, "sib")
        far_work(y * CORES + other, "sib")

    role = None
    for k in ks:
        t = y_tile(k)()
        whole_wait(t, partner)
        to_sib(y_tile(k), beside)
        near_work(t, ("own", k))
        for j in pairs:
            for w in range(2):
                for h in range(BITS):
                    piece_wait(t, ends[w](j), h)
                to_sib(y_tile(k), far(j, w))
        far_work(t, ("own", k))
    for k in ks:
        t = at_y(k) * CORES + other
        for zz in (z, partner):
            whole_wait(t, zz)
        near_work(t, ("sib", k))
        for j in range(2, rows_n):
            whole_wait(t, at_z(j))
        far_work(t, ("sib", k))

    early = list(sent)
    g1t[...] = gacc[...].T.reshape(rows_n, chans // rows_n, band)
    mine = pl.ds(pl.multiple_of(z * band, band), band)
    for k in range(rows_n - 1, 0, -1):
        send(lambda k=k: (g1t.at[at_z(k)], g1_out.at[:, mine], g_send.at[k - 1], g_recv.at[k - 1],
                          {"rows": at_z(k)}))
    g1_out[:, mine] = g1t[z]
    o2[...] = jnp.concatenate([pooled[t, :, :POOL2] for t in range(tiles)], axis=1)
    o3[...] = jnp.concatenate([pooled[t, :, POOL2:POOL2 + POOL3] for t in range(tiles)], axis=1).T
    drain(early)
    some = chans // rows_n // CUTS
    for h in range(CUTS):
        add_y(z, h)
        total = acc[blk, z, h]
        for i in list(range(1, rows_n // 2)) + [0]:
            await_(zin.at[i, h], rz_recv.at[i, h])
            total += zin[i, h]
        g2_out[h * some:(h + 1) * some, :] = total
    for k in range(1, rows_n):
        zz = at_z(k)
        await_(g1_out.at[:, pl.ds(pl.multiple_of(zz * band, band), band)], g_recv.at[k - 1])
    drain(sent[len(early):])


def store(*refs):
    sems = refs[12]
    copies = [pltpu.make_async_copy(refs[i], refs[6 + i], sems.at[i]) for i in range(6)]
    for copy in copies:
        copy.start()
    for copy in copies:
        copy.wait()


def on_device(tiles, rows_n, frame_one, frame_two, cot_zero, cot_one, cot_two, cot_three):
    band, chans = frame_one.shape
    ys_n = tiles // CORES
    part = chans // rows_n
    some = part // CUTS
    cots = (cot_zero, cot_one, cot_two, cot_three)
    hbm = pl.BlockSpec(memory_space=pl.ANY)
    vmem = pl.BlockSpec(memory_space=pltpu.VMEM)
    dma = pltpu.SemaphoreType.DMA
    shapes = tuple(cot.shape for cot in cots[:3]) + (
        cot_three.shape[::-1], (part, band * rows_n), (part, TILE))
    made = pl.pallas_call(
        functools.partial(kernel, tiles, rows_n),
        out_shape=tuple(pltpu.VMEM(shape, f32) for shape in shapes),
        in_specs=[pl.BlockSpec(memory_space=pltpu.HBM)] * 6,
        out_specs=(vmem,) * 6,
        scratch_shapes=[
            pltpu.VMEM((band, chans), f32),
            pltpu.VMEM((tiles * TILE, chans), f32),
            pltpu.VMEM(cot_zero.shape, f32),
            pltpu.VMEM(cot_one.shape, f32),
            pltpu.VMEM(cot_two.shape, f32),
            pltpu.VMEM(cot_three.shape[::-1], f32),
            pltpu.VMEM((tiles, band, POOLED), f32),
            pltpu.VMEM((tiles, 2 * band, TILE), bf16),
            pltpu.VMEM((TILE, POOLED), bf16),
            pltpu.VMEM((2 * band, chans), bf16),
            pltpu.VMEM((chans, 2 * band), bf16),
            pltpu.VMEM((tiles, rows_n, CUTS, some, TILE), f32),
            pltpu.VMEM((ys_n, rows_n, CUTS, some, TILE), f32),
            pltpu.VMEM((ys_n - 1, rows_n, CUTS, some, TILE), f32),
            pltpu.VMEM((rows_n - 2, CUTS, some, TILE), f32),
            pltpu.VMEM((ys_n - 1, CUTS, some, TILE), f32),
            pltpu.VMEM((rows_n // 2, CUTS, some, TILE), f32),
            pltpu.VMEM((tiles, band, POOLED - POOL1), f32),
            pltpu.VMEM((band, chans), f32),
            pltpu.VMEM((rows_n, part, band), f32),
            dma((6,)),
            dma((tiles * rows_n, BITS)),
            dma((rows_n // 2, BITS)),
            dma((ys_n - 1, rows_n, BITS)),
            dma((tiles * rows_n,)),
            dma((ys_n - 1,)),
            dma((rows_n - 2, BITS)),
            dma((ys_n, rows_n // 2 - 1, BITS)),
            dma((ys_n,)), dma((ys_n,)),
            dma((ys_n - 1, rows_n, CUTS)), dma((ys_n - 1, rows_n, CUTS)),
            dma((rows_n - 2, CUTS)), dma((rows_n - 2, CUTS)),
            dma((ys_n - 1, CUTS)), dma((ys_n - 1, CUTS)),
            dma((rows_n - 1, CUTS)), dma((rows_n // 2, CUTS)),
            dma((rows_n - 1,)), dma((rows_n - 1,)),
        ],
        compiler_params=pltpu.CompilerParams(
            collective_id=0, has_side_effects=True, vmem_limit_bytes=48 << 20),
    )(*[pltpu.with_memory_space_constraint(value, pltpu.HBM) for value in (
        frame_one, frame_two, cot_zero, cot_one, cot_two, cot_three.T)])
    placed = pl.pallas_call(
        store,
        out_shape=tuple(jax.ShapeDtypeStruct(shape, f32) for shape in shapes),
        in_specs=[hbm] * 6,
        out_specs=(hbm,) * 6,
        scratch_shapes=[dma((6,))],
        compiler_params=pltpu.CompilerParams(vmem_limit_bytes=1 << 20),
    )(*[pltpu.with_memory_space_constraint(value, pltpu.VMEM) for value in made])
    return placed[:3] + (placed[3].T,) + placed[4:]


def solution(mesh):
    band = P(("groups", "blk", "rows"), None)
    turned = P("rows", ("groups", "blk"))
    return jax.shard_map(
        functools.partial(on_device, mesh.shape["blk"], mesh.shape["rows"]),
        mesh=mesh,
        in_specs=(band,) * 6,
        out_specs=(band,) * 4 + (turned,) * 2,
        check_vma=False,
    )
```

```python
import functools
import math

import jax
import jax.numpy as jnp
from jax import lax
from jax.experimental import pallas as pl
from jax.experimental.pallas import tpu as pltpu
from jax.sharding import PartitionSpec as P

TROWS = 8
W2 = 64
CORES = 2
TILE = TROWS * W2
POOL1 = TILE // 4
POOL2 = TILE // 16
POOL3 = TILE // 64
POOLED = 2 * POOL1
CUTS = 2
BITS = 2

f32 = jnp.float32
bf16 = jnp.bfloat16


def split(x):
    high = x.astype(bf16)
    low = (x - high.astype(f32)).astype(bf16)
    return high, low


def mm(a, b, ca, cb):
    return lax.dot_general(a, b, (((ca,), (cb,)), ((), ())), preferred_element_type=f32)


def pool_table():
    shape = (TILE, POOLED)
    pixel = lax.broadcasted_iota(jnp.int32, (TILE, 1), 0)
    row, col = pixel // W2, pixel % W2
    one = lax.shift_right_logical(row, 1) * (W2 // 2) + lax.shift_right_logical(col, 1)
    two = lax.shift_right_logical(row, 2) * (W2 // 4) + lax.shift_right_logical(col, 2) + POOL1
    three = lax.shift_right_logical(row, 3) * (W2 // 8) + lax.shift_right_logical(col, 3) + (
        POOL1 + POOL2)
    slot = lax.broadcasted_iota(jnp.int32, shape, 1)
    value = jnp.where(slot == one, 0.25, 0.0)
    value = jnp.where(slot == two, 0.0625, value)
    value = jnp.where(slot == three, 0.015625, value)
    return value.astype(bf16)


def kernel(tiles, rows_n, f1_in, f2_in, c0_in, c1_in, c2_in, c3_in,
           o0, o1, o2, o3, g1_out, g2_out,
           f1, f2, c0, c1, c2, c3t, coarse, scaled, table, f1s, f1t, acc, cin, yin, pin, qin, xin, din, zin,
           pooled, gacc, g1t, g1r,
           in_sem, ag_recv, own_send, ys_send, cs_send, zf_send, nf_send, mf_send,
           rc_send, rc_recv, ry_send, ry_recv, rp_send, rp_recv, rq_send, rq_recv, rz_send, rz_recv, rx_recv, rd_recv,
           g_send, g_recv):
    band = f1.shape[0]
    chans = f1.shape[1]
    band2 = f2_in.shape[0]
    ys_n = tiles // CORES
    inv_root = 1.0 / math.sqrt(chans)
    blk = lax.axis_index("blk")
    z = lax.axis_index("rows")
    core = blk % CORES
    y = blk // CORES
    other = 1 - core
    sib = {"blk": y * CORES + other}

    def at_z(k):
        zz, bit = z, 1
        while bit < rows_n:
            if k % (2 * bit) >= bit:
                zz = zz + bit - 2 * bit * (z // bit % 2)
            bit *= 2
        return zz

    def at_y(k):
        return (y + k) % ys_n

    def y_peer(k):
        return {"blk": at_y(k) * CORES + core}

    partner = at_z(1)
    inner = (z + z // 2) % 2 == 1
    outer = (z + z // 2) % 2 == 0
    pairs = range(2, rows_n, 2)

    def far_inner(k):
        pair = at_z(k) // 2
        return pair * 2 + 1 - pair % 2

    def far_outer(k):
        pair = at_z(k) // 2
        return pair * 2 + pair % 2

    def span(t, zz):
        return pl.ds(pl.multiple_of(t * TILE + zz * band2, 8), band2)

    def piece(t, zz, h):
        rows = band2 // BITS
        return pl.ds(pl.multiple_of(t * TILE + zz * band2 + h * rows, 8), rows)

    loads = {}
    for i, (name, src, dst) in enumerate((
            ("f1", f1_in, f1), ("f2", f2_in, f2.at[span(blk, z), :]), ("c3", c3_in, c3t),
            ("c2", c2_in, c2), ("c1", c1_in, c1), ("c0", c0_in, c0))):
        loads[name] = pltpu.make_async_copy(src, dst, in_sem.at[i])
        loads[name].start()

    peers = [{"rows": at_z(k)} for k in range(1, rows_n)]
    peers += [y_peer(k) for k in range(1, ys_n)]
    peers += [sib]
    barrier = pltpu.get_barrier_semaphore()
    for peer in peers:
        pl.semaphore_signal(barrier, inc=1, device_id=peer)
    table[...] = pool_table()
    loads["f2"].wait()
    pl.semaphore_wait(barrier, len(peers))

    sent = []

    def await_(ref, rsem):
        pltpu.make_async_copy(ref, ref, rsem).wait()

    def send(make):
        def copy():
            src, dst, ssem, rsem, peer = make()
            return pltpu.make_async_remote_copy(
                src_ref=src, dst_ref=dst, send_sem=ssem, recv_sem=rsem,
                device_id=peer, device_id_type=pl.DeviceIdType.MESH)

        copy().start()
        sent.append(copy)

    def whole_wait(t, zz):
        await_(f2.at[span(t, zz), :], ag_recv.at[t * rows_n + zz, 0])

    def piece_wait(t, zz, h):
        await_(f2.at[piece(t, zz, h), :], ag_recv.at[t * rows_n + zz, h])

    def whole(t, zz, ssem, peer, src=None):
        where = f2.at[span(t, zz), :]
        return where if src is None else src, where, ssem, ag_recv.at[t * rows_n + zz, 0], peer

    def cut(t, zz, h, ssem, peer, src=None):
        where = f2.at[piece(t, zz, h), :]
        return where if src is None else src, where, ssem, ag_recv.at[t * rows_n + zz, h], peer

    def to_sib(t, zz, src=None):
        send(lambda: whole(t(), zz(), cs_send.at[t() * rows_n + zz()], sib, src))

    def own_tile():
        return blk

    def y_tile(k):
        return lambda: at_y(k) * CORES + core

    def here():
        return z

    def beside():
        return partner

    ks = list(range(1, ys_n))
    ends = (far_inner, far_outer)
    for k in ks:
        send(lambda k=k: whole(blk, z, ys_send.at[k - 1, z, 0], y_peer(k)))
    for h in range(BITS):
        send(lambda h=h: cut(blk, z, h, own_send.at[0, h], {"rows": partner}))
    to_sib(own_tile, here)
    both = list(sent)
    sent.clear()

    @pl.when(inner)
    def _():
        for h in range(BITS):
            for j in pairs:
                send(lambda j=j, h=h: cut(blk, z, h, own_send.at[j // 2, h],
                                          {"rows": far_inner(j)}))

    only_inner = list(sent)
    sent.clear()

    loads["f1"].wait()
    high, low = split(f1[...])
    f1s[0:band, :] = high
    f1s[band:, :] = low
    turned = f1[...].T
    high, low = split(turned)
    f1t[:, 0:band] = high
    f1t[:, band:] = low
    loads["c3"].wait()
    loads["c2"].wait()
    loads["c1"].wait()
    c3 = c3t[...].T
    for t in range(tiles):
        coarse[t] = jnp.concatenate(
            [c1[:, t * POOL1:(t + 1) * POOL1], c2[:, t * POOL2:(t + 1) * POOL2],
             c3[:, t * POOL3:(t + 1) * POOL3],
             jnp.zeros((band, POOLED - POOL1 - POOL2 - POOL3), f32)], axis=1)
    loads["c0"].wait()

    def band_sum(t):
        high, low = split(coarse[t])
        spread = mm(jnp.concatenate([high, low], axis=0), table[...], 1, 1)
        total = c0[:, pl.ds(pl.multiple_of(t * TILE, TILE), TILE)] + (spread[:band] + spread[band:])
        high, low = split(total * inv_root)
        scaled[t, 0:band, :] = high
        scaled[t, band:, :] = low
        twice = jnp.concatenate([high, high], axis=0)
        value = mm(f1t[...], twice, 1, 0) + mm(f1t[:, 0:band], low, 1, 0)
        acc[t] = value.reshape(acc.shape[1:])

    def to_chip(k):
        yy = at_y(k)
        band_sum(yy * CORES + other)
        send(lambda: (acc.at[at_y(k) * CORES + other], cin.at[at_y(k)], rc_send.at[at_y(k)],
                      rc_recv.at[at_y(k)], sib))

    def chip_sum(k):
        yy = at_y(k)
        await_(cin.at[yy], rc_recv.at[yy])
        acc[yy * CORES + core] += cin[yy]

    def sums_to_y(k, zz, hs=range(CUTS)):
        for h in hs:
            send(lambda h=h: (
                acc.at[y_tile(k)(), zz(), h], yin.at[k - 1, zz(), h],
                ry_send.at[k - 1, zz(), h], ry_recv.at[k - 1, zz(), h], y_peer(k)))

    def add_y(zz, h):
        for k in ks:
            await_(yin.at[k - 1, zz, h], ry_recv.at[k - 1, zz, h])
            acc[blk, zz, h] += yin[k - 1, zz, h]

    def far(j, w):
        return lambda: ends[w](j)

    last = CUTS - 1

    for k in ks:
        to_chip(k)
    to_chip(0)
    for k in ks:
        band_sum(y_tile(k)())
        chip_sum(k)
        for j in pairs:
            sums_to_y(k, far(j, 1))
        for j in pairs:
            sums_to_y(k, far(j, 0), range(last))
    band_sum(blk)

    started = []

    def work(t):
        at = pl.ds(pl.multiple_of(t * TILE, TILE), TILE)
        high, low = split(f2[at, :])
        both = mm(f1s[...], high, 1, 1)
        value = (both[:band] + both[band:] + mm(f1s[0:band, :], low, 1, 1)) * inv_root
        o0[:, at] = value
        vh, vl = split(value)
        both = mm(jnp.concatenate([vh, vl], axis=0), table[...], 1, 0)
        both = both[:band] + both[band:]
        pooled[t] = both[:, POOL1:]
        o1[:, pl.ds(pl.multiple_of(t * POOL1, POOL1), POOL1)] = both[:, :POOL1]
        both = mm(scaled[t], high, 1, 0)
        grad = both[:band] + both[band:] + mm(scaled[t, 0:band, :], low, 1, 0)
        if started:
            gacc[...] += grad
        else:
            gacc[...] = grad
        started.append(t)

    def forward(j, w, h, peers, on):
        piece_wait(blk, ends[w](j), h)
        if on:
            send(lambda: cut(blk, ends[w](j), h, nf_send.at[j - 2 + w, h], {"rows": partner}))
        for k in peers:
            send(lambda k=k: cut(blk, ends[w](j), h, ys_send.at[k - 1, ends[w](j), h], y_peer(k)))
        if h == BITS - 1:
            to_sib(own_tile, far(j, w))

    def partner_piece(h, on):
        piece_wait(blk, partner, h)
        if on:
            for j in pairs:
                send(lambda j=j: cut(blk, partner, h, mf_send.at[0, j // 2 - 1, h],
                                     {"rows": far_inner(j)}))
        if h == BITS - 1:
            to_sib(own_tile, beside)

    def y_shard(k, on):
        whole_wait(y_tile(k)(), z)
        if on:
            for h in range(BITS):
                for j in pairs:
                    send(lambda j=j, h=h: cut(y_tile(k)(), z, h, mf_send.at[k, j // 2 - 1, h],
                                              {"rows": far_inner(j)}))
        to_sib(y_tile(k), here)

    def turn(k):
        send(lambda: whole(y_tile(k)(), z, zf_send.at[k - 1], {"rows": partner}))

    def sums(j, w, h, on):
        add_y(ends[w](j), h)
        if on:
            send(lambda: (acc.at[blk, ends[w](j), h], pin.at[j - 2 + w, h],
                          rp_send.at[j - 2 + w, h], rp_recv.at[j - 2 + w, h],
                          {"rows": partner}))

    def combine(j, w, h):
        await_(pin.at[j - 2 + w, h], rp_recv.at[j - 2 + w, h])
        acc[blk, ends[w](j), h] += pin[j - 2 + w, h]
        send(lambda: (acc.at[blk, ends[w](j), h],
                      xin.at[j // 2 - 1, h] if w else zin.at[j // 2, h],
                      rz_send.at[j - 1 + w, h],
                      rx_recv.at[j // 2 - 1, h] if w else rz_recv.at[j // 2, h],
                      {"rows": far_inner(j)}))

    def crossed(h):
        for j in pairs:
            await_(xin.at[j // 2 - 1, h], rx_recv.at[j // 2 - 1, h])
            acc[blk, partner, h] += xin[j // 2 - 1, h]

    def final(h, slots):
        add_y(z, h)
        total = acc[blk, z, h]
        for i in slots:
            await_(zin.at[i, h], rz_recv.at[i, h])
            total += zin[i, h]
            if i and h == last:
                await_(din.at[i - 1], rd_recv.at[i - 1])
                total += din[i - 1]
        some = chans // rows_n // CUTS
        g2_out[h * some:(h + 1) * some, :] = total

    def direct(j, is_inner):
        add_y(far_inner(j), last)
        send(lambda: (acc.at[blk, far_inner(j), last],
                      zin.at[j // 2, last] if is_inner else din.at[j // 2 - 1],
                      rz_send.at[j - 1, last],
                      rz_recv.at[j // 2, last] if is_inner else rd_recv.at[j // 2 - 1],
                      {"rows": far_inner(j)}))

    def partner_sums(h):
        send(lambda: (acc.at[blk, partner, h], zin.at[0, h], rz_send.at[0, h], rz_recv.at[0, h],
                      {"rows": partner}))

    def sib_wait():
        for zz in range(rows_n):
            whole_wait(y * CORES + other, zz)

    bits = [[(j, w, h) for j in pairs for h in range(BITS)] for w in range(2)]
    late = []
    both += sent
    sent.clear()
    mine = pl.ds(pl.multiple_of(z * band, band), band)

    def y_tiles(between):
        late.append(len(sent))
        for k in ks:
            t = y_tile(k)()
            whole_wait(t, partner)
            to_sib(y_tile(k), beside)
            for j in pairs:
                for w in range(2):
                    for h in range(BITS):
                        piece_wait(t, ends[w](j), h)
                    to_sib(y_tile(k), far(j, w))
            work(t)
        between()
        for k in ks:
            t = at_y(k) * CORES + other
            for zz in range(rows_n):
                whole_wait(t, zz)
            work(t)
        g1t[...] = gacc[...].T.reshape(rows_n, chans // rows_n, band)
        for k in range(rows_n - 1, 0, -1):
            send(lambda k=k: (g1t.at[at_z(k)], g1r.at[k - 1], g_send.at[k - 1],
                              g_recv.at[k - 1], {"rows": at_z(k)}))
        g1_out[:, mine] = g1t[z]

    halves = [(j, w, h) for j in pairs for w in range(2) for h in range(CUTS)]
    inners = [(j, w, h) for j, w, h in halves if w == 0 and h < last]
    outers = [(j, w, h) for j, w, h in halves if w == 1]

    def finish(slots, first):
        o2[...] = jnp.concatenate([pooled[t, :, :POOL2] for t in range(tiles)], axis=1)
        o3[...] = jnp.concatenate(
            [pooled[t, :, POOL2:POOL2 + POOL3] for t in range(tiles)], axis=1).T
        for copy in first + sent[:late[-1]]:
            copy().wait_send()
        for h in range(CUTS):
            final(h, slots)
        for k in range(1, rows_n):
            await_(g1r.at[k - 1], g_recv.at[k - 1])
            at = pl.multiple_of(at_z(k) * band, band)
            g1_out[:, pl.ds(at, band)] = g1r[k - 1]
        for copy in sent[late[-1]:]:
            copy().wait_send()


    @pl.when(inner)
    def _():
        for k in ks:
            sums_to_y(k, beside, range(last))
        partner_piece(0, True)
        for j, w, h in bits[0]:
            if h and j == 2:
                partner_piece(h, True)
            forward(j, w, h, [], True)
        for k in ks:
            y_shard(k, True)
        for j, w, h in bits[1]:
            forward(j, w, h, ks, True)
        for k in ks:
            turn(k)
            sums_to_y(k, beside, [last])
            for j in pairs:
                sums_to_y(k, far(j, 0), [last])
        for k in ks:
            for h in range(CUTS):
                await_(qin.at[k - 1, h], rq_recv.at[k - 1, h])
                acc[y_tile(k)(), z, h] += qin[k - 1, h]
            sums_to_y(k, here)
        chip_sum(0)
        for j, w, h in outers:
            sums(j, w, h, False)
        for j, w, h in inners:
            sums(j, w, h, False)
        work(blk)
        combine(*outers[0])
        sib_wait()
        work(y * CORES + other)
        for j, w, h in outers[1:]:
            combine(j, w, h)
        def rest(h):
            for j, w, hh in inners:
                if hh == h:
                    combine(j, w, h)
            add_y(partner, h)
            crossed(h)
            partner_sums(h)

        y_tiles(lambda: None)
        for h in range(CUTS):
            rest(h)
        for j in pairs:
            direct(j, True)
        finish(range(rows_n // 2), both + only_inner)

    started.clear()
    sent.clear()

    @pl.when(outer)
    def _():
        for k in ks:
            for h in range(CUTS):
                send(lambda k=k, h=h: (
                    acc.at[y_tile(k)(), partner, h], qin.at[k - 1, h], rq_send.at[k - 1, h],
                    rq_recv.at[k - 1, h], {"rows": partner}))
        for h in range(BITS):
            partner_piece(h, False)
        for k in ks:
            y_shard(k, False)
            turn(k)
        chip_sum(0)
        step = BITS // CUTS
        for w in (1, 0):
            for h in range(CUTS):
                for j in pairs:
                    if w or h < last:
                        sums(j, w, h, True)
                for j in pairs:
                    for b in range(h * step, h * step + step):
                        forward(j, 1 - w, b, ks, False)
        for k in ks:
            for j in pairs:
                sums_to_y(k, far(j, 0), [last])
            sums_to_y(k, here)
        for h in range(CUTS):
            partner_sums(h)
        work(blk)
        sib_wait()
        work(y * CORES + other)
        y_tiles(lambda: [direct(j, False) for j in pairs])
        finish([0], both)


def store(*refs):
    sems = refs[12]
    copies = [pltpu.make_async_copy(refs[i], refs[6 + i], sems.at[i]) for i in range(6)]
    for copy in copies:
        copy.start()
    for copy in copies:
        copy.wait()


def on_device(tiles, rows_n, frame_one, frame_two, cot_zero, cot_one, cot_two, cot_three):
    band, chans = frame_one.shape
    ys_n = tiles // CORES
    part = chans // rows_n
    some = part // CUTS
    cots = (cot_zero, cot_one, cot_two, cot_three)
    hbm = pl.BlockSpec(memory_space=pl.ANY)
    vmem = pl.BlockSpec(memory_space=pltpu.VMEM)
    dma = pltpu.SemaphoreType.DMA
    shapes = tuple(cot.shape for cot in cots[:3]) + (
        cot_three.shape[::-1], (part, band * rows_n), (part, TILE))
    made = pl.pallas_call(
        functools.partial(kernel, tiles, rows_n),
        out_shape=tuple(pltpu.VMEM(shape, f32) for shape in shapes),
        in_specs=[pl.BlockSpec(memory_space=pltpu.HBM)] * 6,
        out_specs=(vmem,) * 6,
        scratch_shapes=[
            pltpu.VMEM((band, chans), f32),
            pltpu.VMEM((tiles * TILE, chans), f32),
            pltpu.VMEM(cot_zero.shape, f32),
            pltpu.VMEM(cot_one.shape, f32),
            pltpu.VMEM(cot_two.shape, f32),
            pltpu.VMEM(cot_three.shape[::-1], f32),
            pltpu.VMEM((tiles, band, POOLED), f32),
            pltpu.VMEM((tiles, 2 * band, TILE), bf16),
            pltpu.VMEM((TILE, POOLED), bf16),
            pltpu.VMEM((2 * band, chans), bf16),
            pltpu.VMEM((chans, 2 * band), bf16),
            pltpu.VMEM((tiles, rows_n, CUTS, some, TILE), f32),
            pltpu.VMEM((ys_n, rows_n, CUTS, some, TILE), f32),
            pltpu.VMEM((ys_n - 1, rows_n, CUTS, some, TILE), f32),
            pltpu.VMEM((rows_n - 2, CUTS, some, TILE), f32),
            pltpu.VMEM((ys_n - 1, CUTS, some, TILE), f32),
            pltpu.VMEM((rows_n // 2 - 1, CUTS, some, TILE), f32),
            pltpu.VMEM((rows_n // 2 - 1, some, TILE), f32),
            pltpu.VMEM((rows_n // 2, CUTS, some, TILE), f32),
            pltpu.VMEM((tiles, band, POOLED - POOL1), f32),
            pltpu.VMEM((band, chans), f32),
            pltpu.VMEM((rows_n, part, band), f32),
            pltpu.VMEM((rows_n - 1, part, band), f32),
            dma((6,)),
            dma((tiles * rows_n, BITS)),
            dma((rows_n // 2, BITS)),
            dma((ys_n - 1, rows_n, BITS)),
            dma((tiles * rows_n,)),
            dma((ys_n - 1,)),
            dma((rows_n - 2, BITS)),
            dma((ys_n, rows_n // 2 - 1, BITS)),
            dma((ys_n,)), dma((ys_n,)),
            dma((ys_n - 1, rows_n, CUTS)), dma((ys_n - 1, rows_n, CUTS)),
            dma((rows_n - 2, CUTS)), dma((rows_n - 2, CUTS)),
            dma((ys_n - 1, CUTS)), dma((ys_n - 1, CUTS)),
            dma((rows_n - 1, CUTS)), dma((rows_n // 2, CUTS)), dma((rows_n // 2 - 1, CUTS)),
            dma((rows_n // 2 - 1,)),
            dma((rows_n - 1,)), dma((rows_n - 1,)),
        ],
        compiler_params=pltpu.CompilerParams(
            collective_id=0, has_side_effects=True, vmem_limit_bytes=48 << 20),
    )(*[pltpu.with_memory_space_constraint(value, pltpu.HBM) for value in (
        frame_one, frame_two, cot_zero, cot_one, cot_two, cot_three.T)])
    placed = pl.pallas_call(
        store,
        out_shape=tuple(jax.ShapeDtypeStruct(shape, f32) for shape in shapes),
        in_specs=[hbm] * 6,
        out_specs=(hbm,) * 6,
        scratch_shapes=[dma((6,))],
        compiler_params=pltpu.CompilerParams(vmem_limit_bytes=1 << 20),
    )(*[pltpu.with_memory_space_constraint(value, pltpu.VMEM) for value in made])
    return placed[:3] + (placed[3].T,) + placed[4:]


def solution(mesh):
    band = P(("groups", "blk", "rows"), None)
    turned = P("rows", ("groups", "blk"))
    return jax.shard_map(
        functools.partial(on_device, mesh.shape["blk"], mesh.shape["rows"]),
        mesh=mesh,
        in_specs=(band,) * 6,
        out_specs=(band,) * 4 + (turned,) * 2,
        check_vma=False,
    )
```

```python
import functools
import math

import jax
import jax.numpy as jnp
from jax import lax
from jax.experimental import pallas as pl
from jax.experimental.pallas import tpu as pltpu
from jax.sharding import PartitionSpec as P

TROWS = 8
W2 = 64
CORES = 2
TILE = TROWS * W2
POOL1 = TILE // 4
POOL2 = TILE // 16
POOL3 = TILE // 64
POOLED = 2 * POOL1
CUTS = 2
BITS = 2

f32 = jnp.float32
bf16 = jnp.bfloat16


def split(x):
    high = x.astype(bf16)
    low = (x - high.astype(f32)).astype(bf16)
    return high, low


def mm(a, b, ca, cb):
    return lax.dot_general(a, b, (((ca,), (cb,)), ((), ())), preferred_element_type=f32)


def pool_table():
    shape = (TILE, POOLED)
    pixel = lax.broadcasted_iota(jnp.int32, (TILE, 1), 0)
    row, col = pixel // W2, pixel % W2
    one = lax.shift_right_logical(row, 1) * (W2 // 2) + lax.shift_right_logical(col, 1)
    two = lax.shift_right_logical(row, 2) * (W2 // 4) + lax.shift_right_logical(col, 2) + POOL1
    three = lax.shift_right_logical(row, 3) * (W2 // 8) + lax.shift_right_logical(col, 3) + (
        POOL1 + POOL2)
    slot = lax.broadcasted_iota(jnp.int32, shape, 1)
    value = jnp.where(slot == one, 0.25, 0.0)
    value = jnp.where(slot == two, 0.0625, value)
    value = jnp.where(slot == three, 0.015625, value)
    return value.astype(bf16)


def kernel(tiles, rows_n, f1_in, f2_in, c0_in, c1_in, c2_in, c3_in,
           o0, o1, o2, o3, g1_out, g2_out,
           f1, f2, c0, c1, c2, c3t, coarse, scaled, table, f1s, f1t, acc, cin, yin, pin, qin, xin, din, zin,
           pooled, gacc, g1t, g1r,
           in_sem, ag_recv, own_send, ys_send, cs_send, zf_send, nf_send, mf_send,
           rc_send, rc_recv, ry_send, ry_recv, rp_send, rp_recv, rq_send, rq_recv, rz_send, rz_recv, rx_recv, rd_recv,
           g_send, g_recv):
    band = f1.shape[0]
    chans = f1.shape[1]
    band2 = f2_in.shape[0]
    ys_n = tiles // CORES
    inv_root = 1.0 / math.sqrt(chans)
    blk = lax.axis_index("blk")
    z = lax.axis_index("rows")
    core = blk % CORES
    y = blk // CORES
    other = 1 - core
    sib = {"blk": y * CORES + other}

    def at_z(k):
        zz, bit = z, 1
        while bit < rows_n:
            if k % (2 * bit) >= bit:
                zz = zz + bit - 2 * bit * (z // bit % 2)
            bit *= 2
        return zz

    def at_y(k):
        return (y + k) % ys_n

    def y_peer(k):
        return {"blk": at_y(k) * CORES + core}

    partner = at_z(1)
    inner = (z + z // 2) % 2 == 1
    outer = (z + z // 2) % 2 == 0
    pairs = range(2, rows_n, 2)

    def far_inner(k):
        pair = at_z(k) // 2
        return pair * 2 + 1 - pair % 2

    def far_outer(k):
        pair = at_z(k) // 2
        return pair * 2 + pair % 2

    def span(t, zz):
        return pl.ds(pl.multiple_of(t * TILE + zz * band2, 8), band2)

    def piece(t, zz, h):
        rows = band2 // BITS
        return pl.ds(pl.multiple_of(t * TILE + zz * band2 + h * rows, 8), rows)

    loads = {}
    for i, (name, src, dst) in enumerate((
            ("f1", f1_in, f1), ("f2", f2_in, f2.at[span(blk, z), :]), ("c3", c3_in, c3t),
            ("c2", c2_in, c2), ("c1", c1_in, c1), ("c0", c0_in, c0))):
        loads[name] = pltpu.make_async_copy(src, dst, in_sem.at[i])
        loads[name].start()

    peers = [{"rows": at_z(k)} for k in range(1, rows_n)]
    peers += [y_peer(k) for k in range(1, ys_n)]
    peers += [sib]
    barrier = pltpu.get_barrier_semaphore()
    for peer in peers:
        pl.semaphore_signal(barrier, inc=1, device_id=peer)
    table[...] = pool_table()
    loads["f2"].wait()
    pl.semaphore_wait(barrier, len(peers))

    sent = []

    def await_(ref, rsem):
        pltpu.make_async_copy(ref, ref, rsem).wait()

    def send(make):
        def copy():
            src, dst, ssem, rsem, peer = make()
            return pltpu.make_async_remote_copy(
                src_ref=src, dst_ref=dst, send_sem=ssem, recv_sem=rsem,
                device_id=peer, device_id_type=pl.DeviceIdType.MESH)

        copy().start()
        sent.append(copy)

    def whole_wait(t, zz):
        await_(f2.at[span(t, zz), :], ag_recv.at[t * rows_n + zz, 0])

    def piece_wait(t, zz, h):
        await_(f2.at[piece(t, zz, h), :], ag_recv.at[t * rows_n + zz, h])

    def whole(t, zz, ssem, peer, src=None):
        where = f2.at[span(t, zz), :]
        return where if src is None else src, where, ssem, ag_recv.at[t * rows_n + zz, 0], peer

    def cut(t, zz, h, ssem, peer, src=None):
        where = f2.at[piece(t, zz, h), :]
        return where if src is None else src, where, ssem, ag_recv.at[t * rows_n + zz, h], peer

    def to_sib(t, zz, src=None):
        send(lambda: whole(t(), zz(), cs_send.at[t() * rows_n + zz()], sib, src))

    def own_tile():
        return blk

    def y_tile(k):
        return lambda: at_y(k) * CORES + core

    def here():
        return z

    def beside():
        return partner

    ks = list(range(1, ys_n))
    ends = (far_inner, far_outer)
    for k in ks:
        send(lambda k=k: whole(blk, z, ys_send.at[k - 1, z, 0], y_peer(k)))
    for h in range(BITS):
        send(lambda h=h: cut(blk, z, h, own_send.at[0, h], {"rows": partner}))
    to_sib(own_tile, here)
    both = list(sent)
    sent.clear()

    @pl.when(inner)
    def _():
        for h in range(BITS):
            for j in pairs:
                send(lambda j=j, h=h: cut(blk, z, h, own_send.at[j // 2, h],
                                          {"rows": far_inner(j)}))

    only_inner = list(sent)
    sent.clear()

    loads["f1"].wait()
    high, low = split(f1[...])
    f1s[0:band, :] = high
    f1s[band:, :] = low
    turned = f1[...].T
    high, low = split(turned)
    f1t[:, 0:band] = high
    f1t[:, band:] = low
    loads["c3"].wait()
    loads["c2"].wait()
    loads["c1"].wait()
    c3 = c3t[...].T
    for t in range(tiles):
        coarse[t] = jnp.concatenate(
            [c1[:, t * POOL1:(t + 1) * POOL1], c2[:, t * POOL2:(t + 1) * POOL2],
             c3[:, t * POOL3:(t + 1) * POOL3],
             jnp.zeros((band, POOLED - POOL1 - POOL2 - POOL3), f32)], axis=1)
    loads["c0"].wait()

    def band_sum(t):
        high, low = split(coarse[t])
        spread = mm(jnp.concatenate([high, low], axis=0), table[...], 1, 1)
        total = c0[:, pl.ds(pl.multiple_of(t * TILE, TILE), TILE)] + (spread[:band] + spread[band:])
        high, low = split(total * inv_root)
        scaled[t, 0:band, :] = high
        scaled[t, band:, :] = low
        twice = jnp.concatenate([high, high], axis=0)
        value = mm(f1t[...], twice, 1, 0) + mm(f1t[:, 0:band], low, 1, 0)
        acc[t] = value.reshape(acc.shape[1:])

    def to_chip(k):
        yy = at_y(k)
        band_sum(yy * CORES + other)
        send(lambda: (acc.at[at_y(k) * CORES + other], cin.at[at_y(k)], rc_send.at[at_y(k)],
                      rc_recv.at[at_y(k)], sib))

    def chip_sum(k):
        yy = at_y(k)
        await_(cin.at[yy], rc_recv.at[yy])
        acc[yy * CORES + core] += cin[yy]

    def sums_to_y(k, zz, hs=range(CUTS)):
        for h in hs:
            send(lambda h=h: (
                acc.at[y_tile(k)(), zz(), h], yin.at[k - 1, zz(), h],
                ry_send.at[k - 1, zz(), h], ry_recv.at[k - 1, zz(), h], y_peer(k)))

    def add_y(zz, h):
        for k in ks:
            await_(yin.at[k - 1, zz, h], ry_recv.at[k - 1, zz, h])
            acc[blk, zz, h] += yin[k - 1, zz, h]

    def far(j, w):
        return lambda: ends[w](j)

    last = CUTS - 1

    for k in ks:
        to_chip(k)
    to_chip(0)
    for k in ks:
        band_sum(y_tile(k)())
        if k == ks[-1]:
            band_sum(blk)
        chip_sum(k)
        for j in pairs:
            sums_to_y(k, far(j, 1))
        for j in pairs:
            sums_to_y(k, far(j, 0), range(last))

    started = []

    def work(t):
        at = pl.ds(pl.multiple_of(t * TILE, TILE), TILE)
        high, low = split(f2[at, :])
        both = mm(f1s[...], high, 1, 1)
        value = (both[:band] + both[band:] + mm(f1s[0:band, :], low, 1, 1)) * inv_root
        o0[:, at] = value
        vh, vl = split(value)
        both = mm(jnp.concatenate([vh, vl], axis=0), table[...], 1, 0)
        both = both[:band] + both[band:]
        pooled[t] = both[:, POOL1:]
        o1[:, pl.ds(pl.multiple_of(t * POOL1, POOL1), POOL1)] = both[:, :POOL1]
        both = mm(scaled[t], high, 1, 0)
        grad = both[:band] + both[band:] + mm(scaled[t, 0:band, :], low, 1, 0)
        if started:
            gacc[...] += grad
        else:
            gacc[...] = grad
        started.append(t)

    def forward(j, w, h, peers, on):
        piece_wait(blk, ends[w](j), h)
        if on:
            send(lambda: cut(blk, ends[w](j), h, nf_send.at[j - 2 + w, h], {"rows": partner}))
        for k in peers:
            send(lambda k=k: cut(blk, ends[w](j), h, ys_send.at[k - 1, ends[w](j), h], y_peer(k)))
        if h == BITS - 1:
            to_sib(own_tile, far(j, w))

    def partner_piece(h, on):
        piece_wait(blk, partner, h)
        if on:
            for j in pairs:
                send(lambda j=j: cut(blk, partner, h, mf_send.at[0, j // 2 - 1, h],
                                     {"rows": far_inner(j)}))
        if h == BITS - 1:
            to_sib(own_tile, beside)

    def y_shard(k, on):
        whole_wait(y_tile(k)(), z)
        if on:
            for h in range(BITS):
                for j in pairs:
                    send(lambda j=j, h=h: cut(y_tile(k)(), z, h, mf_send.at[k, j // 2 - 1, h],
                                              {"rows": far_inner(j)}))
        to_sib(y_tile(k), here)

    def turn(k):
        send(lambda: whole(y_tile(k)(), z, zf_send.at[k - 1], {"rows": partner}))

    def sums(j, w, h, on):
        add_y(ends[w](j), h)
        if on:
            send(lambda: (acc.at[blk, ends[w](j), h], pin.at[j - 2 + w, h],
                          rp_send.at[j - 2 + w, h], rp_recv.at[j - 2 + w, h],
                          {"rows": partner}))

    def combine(j, w, h):
        await_(pin.at[j - 2 + w, h], rp_recv.at[j - 2 + w, h])
        acc[blk, ends[w](j), h] += pin[j - 2 + w, h]
        send(lambda: (acc.at[blk, ends[w](j), h],
                      xin.at[j // 2 - 1, h] if w else zin.at[j // 2, h],
                      rz_send.at[j - 1 + w, h],
                      rx_recv.at[j // 2 - 1, h] if w else rz_recv.at[j // 2, h],
                      {"rows": far_inner(j)}))

    def crossed(h):
        for j in pairs:
            await_(xin.at[j // 2 - 1, h], rx_recv.at[j // 2 - 1, h])
            acc[blk, partner, h] += xin[j // 2 - 1, h]

    def final(h, slots):
        add_y(z, h)
        total = acc[blk, z, h]
        for i in slots:
            await_(zin.at[i, h], rz_recv.at[i, h])
            total += zin[i, h]
            if i and h == last:
                await_(din.at[i - 1], rd_recv.at[i - 1])
                total += din[i - 1]
        some = chans // rows_n // CUTS
        g2_out[h * some:(h + 1) * some, :] = total

    def direct(j, is_inner):
        add_y(far_inner(j), last)
        send(lambda: (acc.at[blk, far_inner(j), last],
                      zin.at[j // 2, last] if is_inner else din.at[j // 2 - 1],
                      rz_send.at[j - 1, last],
                      rz_recv.at[j // 2, last] if is_inner else rd_recv.at[j // 2 - 1],
                      {"rows": far_inner(j)}))

    def partner_sums(h):
        send(lambda: (acc.at[blk, partner, h], zin.at[0, h], rz_send.at[0, h], rz_recv.at[0, h],
                      {"rows": partner}))

    def sib_wait():
        for zz in range(rows_n):
            whole_wait(y * CORES + other, zz)

    bits = [[(j, w, h) for j in pairs for h in range(BITS)] for w in range(2)]
    late = []
    both += sent
    sent.clear()
    mine = pl.ds(pl.multiple_of(z * band, band), band)

    def y_tiles(between):
        late.append(len(sent))
        for k in ks:
            t = y_tile(k)()
            whole_wait(t, partner)
            to_sib(y_tile(k), beside)
            for j in pairs:
                for w in range(2):
                    for h in range(BITS):
                        piece_wait(t, ends[w](j), h)
                    to_sib(y_tile(k), far(j, w))
            work(t)
        between()
        for k in ks:
            t = at_y(k) * CORES + other
            for zz in range(rows_n):
                whole_wait(t, zz)
            work(t)
        g1t[...] = gacc[...].T.reshape(rows_n, chans // rows_n, band)
        for k in range(rows_n - 1, 0, -1):
            send(lambda k=k: (g1t.at[at_z(k)], g1r.at[k - 1], g_send.at[k - 1],
                              g_recv.at[k - 1], {"rows": at_z(k)}))
        g1_out[:, mine] = g1t[z]

    halves = [(j, w, h) for j in pairs for w in range(2) for h in range(CUTS)]
    inners = [(j, w, h) for j, w, h in halves if w == 0 and h < last]
    outers = [(j, w, h) for j, w, h in halves if w == 1]

    def finish(slots, first):
        o2[...] = jnp.concatenate([pooled[t, :, :POOL2] for t in range(tiles)], axis=1)
        o3[...] = jnp.concatenate(
            [pooled[t, :, POOL2:POOL2 + POOL3] for t in range(tiles)], axis=1).T
        for copy in first + sent[:late[-1]]:
            copy().wait_send()
        for h in range(CUTS):
            final(h, slots)
        for k in range(1, rows_n):
            await_(g1r.at[k - 1], g_recv.at[k - 1])
            at = pl.multiple_of(at_z(k) * band, band)
            g1_out[:, pl.ds(at, band)] = g1r[k - 1]
        for copy in sent[late[-1]:]:
            copy().wait_send()


    @pl.when(inner)
    def _():
        for k in ks:
            sums_to_y(k, beside, range(last))
        partner_piece(0, True)
        for j, w, h in bits[0]:
            if h and j == 2:
                partner_piece(h, True)
            forward(j, w, h, [], True)
        for k in ks:
            y_shard(k, True)
        for j, w, h in bits[1]:
            forward(j, w, h, ks, True)
        for k in ks:
            turn(k)
            sums_to_y(k, beside, [last])
            for j in pairs:
                sums_to_y(k, far(j, 0), [last])
        for k in ks:
            for h in range(CUTS):
                await_(qin.at[k - 1, h], rq_recv.at[k - 1, h])
                acc[y_tile(k)(), z, h] += qin[k - 1, h]
            sums_to_y(k, here)
        chip_sum(0)
        for j, w, h in outers:
            sums(j, w, h, False)
        for j, w, h in inners:
            sums(j, w, h, False)
        work(blk)
        combine(*outers[0])
        sib_wait()
        work(y * CORES + other)
        for j, w, h in outers[1:]:
            combine(j, w, h)
        def rest(h):
            add_y(partner, h)
            crossed(h)
            partner_sums(h)

        y_tiles(lambda: [combine(*item) for item in inners])
        for h in range(CUTS):
            rest(h)
        for j in pairs:
            direct(j, True)
        finish(range(rows_n // 2), both + only_inner)

    started.clear()
    sent.clear()

    @pl.when(outer)
    def _():
        for k in ks:
            for h in range(CUTS):
                send(lambda k=k, h=h: (
                    acc.at[y_tile(k)(), partner, h], qin.at[k - 1, h], rq_send.at[k - 1, h],
                    rq_recv.at[k - 1, h], {"rows": partner}))
        for h in range(BITS):
            partner_piece(h, False)
        for k in ks:
            y_shard(k, False)
            turn(k)
        chip_sum(0)
        step = BITS // CUTS
        for w in (1, 0):
            for h in range(CUTS):
                for j in pairs:
                    if w or h < last:
                        sums(j, w, h, True)
                for j in pairs:
                    for b in range(h * step, h * step + step):
                        forward(j, 1 - w, b, ks, False)
        for k in ks:
            for j in pairs:
                sums_to_y(k, far(j, 0), [last])
            sums_to_y(k, here)
        for h in range(CUTS):
            partner_sums(h)
        work(blk)
        y_tiles(lambda: [direct(j, False) for j in pairs] + [sib_wait(), work(y * CORES + other)])
        finish([0], both)


def store(*refs):
    sems = refs[12]
    copies = [pltpu.make_async_copy(refs[i], refs[6 + i], sems.at[i]) for i in range(6)]
    for copy in copies:
        copy.start()
    for copy in copies:
        copy.wait()


def on_device(tiles, rows_n, frame_one, frame_two, cot_zero, cot_one, cot_two, cot_three):
    band, chans = frame_one.shape
    ys_n = tiles // CORES
    part = chans // rows_n
    some = part // CUTS
    cots = (cot_zero, cot_one, cot_two, cot_three)
    hbm = pl.BlockSpec(memory_space=pl.ANY)
    vmem = pl.BlockSpec(memory_space=pltpu.VMEM)
    dma = pltpu.SemaphoreType.DMA
    shapes = tuple(cot.shape for cot in cots[:3]) + (
        cot_three.shape[::-1], (part, band * rows_n), (part, TILE))
    made = pl.pallas_call(
        functools.partial(kernel, tiles, rows_n),
        out_shape=tuple(pltpu.VMEM(shape, f32) for shape in shapes),
        in_specs=[pl.BlockSpec(memory_space=pltpu.HBM)] * 6,
        out_specs=(vmem,) * 6,
        scratch_shapes=[
            pltpu.VMEM((band, chans), f32),
            pltpu.VMEM((tiles * TILE, chans), f32),
            pltpu.VMEM(cot_zero.shape, f32),
            pltpu.VMEM(cot_one.shape, f32),
            pltpu.VMEM(cot_two.shape, f32),
            pltpu.VMEM(cot_three.shape[::-1], f32),
            pltpu.VMEM((tiles, band, POOLED), f32),
            pltpu.VMEM((tiles, 2 * band, TILE), bf16),
            pltpu.VMEM((TILE, POOLED), bf16),
            pltpu.VMEM((2 * band, chans), bf16),
            pltpu.VMEM((chans, 2 * band), bf16),
            pltpu.VMEM((tiles, rows_n, CUTS, some, TILE), f32),
            pltpu.VMEM((ys_n, rows_n, CUTS, some, TILE), f32),
            pltpu.VMEM((ys_n - 1, rows_n, CUTS, some, TILE), f32),
            pltpu.VMEM((rows_n - 2, CUTS, some, TILE), f32),
            pltpu.VMEM((ys_n - 1, CUTS, some, TILE), f32),
            pltpu.VMEM((rows_n // 2 - 1, CUTS, some, TILE), f32),
            pltpu.VMEM((rows_n // 2 - 1, some, TILE), f32),
            pltpu.VMEM((rows_n // 2, CUTS, some, TILE), f32),
            pltpu.VMEM((tiles, band, POOLED - POOL1), f32),
            pltpu.VMEM((band, chans), f32),
            pltpu.VMEM((rows_n, part, band), f32),
            pltpu.VMEM((rows_n - 1, part, band), f32),
            dma((6,)),
            dma((tiles * rows_n, BITS)),
            dma((rows_n // 2, BITS)),
            dma((ys_n - 1, rows_n, BITS)),
            dma((tiles * rows_n,)),
            dma((ys_n - 1,)),
            dma((rows_n - 2, BITS)),
            dma((ys_n, rows_n // 2 - 1, BITS)),
            dma((ys_n,)), dma((ys_n,)),
            dma((ys_n - 1, rows_n, CUTS)), dma((ys_n - 1, rows_n, CUTS)),
            dma((rows_n - 2, CUTS)), dma((rows_n - 2, CUTS)),
            dma((ys_n - 1, CUTS)), dma((ys_n - 1, CUTS)),
            dma((rows_n - 1, CUTS)), dma((rows_n // 2, CUTS)), dma((rows_n // 2 - 1, CUTS)),
            dma((rows_n // 2 - 1,)),
            dma((rows_n - 1,)), dma((rows_n - 1,)),
        ],
        compiler_params=pltpu.CompilerParams(
            collective_id=0, has_side_effects=True, vmem_limit_bytes=48 << 20),
    )(*[pltpu.with_memory_space_constraint(value, pltpu.HBM) for value in (
        frame_one, frame_two, cot_zero, cot_one, cot_two, cot_three.T)])
    placed = pl.pallas_call(
        store,
        out_shape=tuple(jax.ShapeDtypeStruct(shape, f32) for shape in shapes),
        in_specs=[hbm] * 6,
        out_specs=(hbm,) * 6,
        scratch_shapes=[dma((6,))],
        compiler_params=pltpu.CompilerParams(vmem_limit_bytes=1 << 20),
    )(*[pltpu.with_memory_space_constraint(value, pltpu.VMEM) for value in made])
    return placed[:3] + (placed[3].T,) + placed[4:]


def solution(mesh):
    band = P(("groups", "blk", "rows"), None)
    turned = P("rows", ("groups", "blk"))
    return jax.shard_map(
        functools.partial(on_device, mesh.shape["blk"], mesh.shape["rows"]),
        mesh=mesh,
        in_specs=(band,) * 6,
        out_specs=(band,) * 4 + (turned,) * 2,
        check_vma=False,
    )
```

```python
import functools
import math

import jax
import jax.numpy as jnp
from jax import lax
from jax.experimental import pallas as pl
from jax.experimental.pallas import tpu as pltpu
from jax.sharding import PartitionSpec as P

TROWS = 8
W2 = 64
CORES = 2
TILE = TROWS * W2
POOL1 = TILE // 4
POOL2 = TILE // 16
POOL3 = TILE // 64
POOLED = 2 * POOL1
CUTS = 2
BITS = 2

f32 = jnp.float32
bf16 = jnp.bfloat16


def split(x):
    high = x.astype(bf16)
    low = (x - high.astype(f32)).astype(bf16)
    return high, low


def mm(a, b, ca, cb):
    return lax.dot_general(a, b, (((ca,), (cb,)), ((), ())), preferred_element_type=f32)


def pool_table():
    shape = (TILE, POOLED)
    pixel = lax.broadcasted_iota(jnp.int32, (TILE, 1), 0)
    row, col = pixel // W2, pixel % W2
    one = lax.shift_right_logical(row, 1) * (W2 // 2) + lax.shift_right_logical(col, 1)
    two = lax.shift_right_logical(row, 2) * (W2 // 4) + lax.shift_right_logical(col, 2) + POOL1
    three = lax.shift_right_logical(row, 3) * (W2 // 8) + lax.shift_right_logical(col, 3) + (
        POOL1 + POOL2)
    slot = lax.broadcasted_iota(jnp.int32, shape, 1)
    value = jnp.where(slot == one, 0.25, 0.0)
    value = jnp.where(slot == two, 0.0625, value)
    value = jnp.where(slot == three, 0.015625, value)
    return value.astype(bf16)


def kernel(tiles, rows_n, f1_in, f2_in, c0_in, c1_in, c2_in, c3_in,
           o0, o1, o2, o3, g1_out, g2_out,
           f1, f2, c0, c1, c2, c3t, coarse, scaled, table, f1s, f1t, acc, cin, yin, pin, qin, xin, din, zin,
           pooled, gacc, g1t, g1r,
           in_sem, ag_recv, own_send, ys_send, cs_send, zf_send, nf_send, mf_send,
           rc_send, rc_recv, ry_send, ry_recv, rp_send, rp_recv, rq_send, rq_recv, rz_send, rz_recv, rx_recv, rd_recv,
           g_send, g_recv):
    band = f1.shape[0]
    chans = f1.shape[1]
    band2 = f2_in.shape[0]
    ys_n = tiles // CORES
    inv_root = 1.0 / math.sqrt(chans)
    blk = lax.axis_index("blk")
    z = lax.axis_index("rows")
    core = blk % CORES
    y = blk // CORES
    other = 1 - core
    sib = {"blk": y * CORES + other}

    def at_z(k):
        zz, bit = z, 1
        while bit < rows_n:
            if k % (2 * bit) >= bit:
                zz = zz + bit - 2 * bit * (z // bit % 2)
            bit *= 2
        return zz

    def at_y(k):
        return (y + k) % ys_n

    def y_peer(k):
        return {"blk": at_y(k) * CORES + core}

    partner = at_z(1)
    inner = (z + z // 2) % 2 == 1
    outer = (z + z // 2) % 2 == 0
    pairs = range(2, rows_n, 2)

    def far_inner(k):
        pair = at_z(k) // 2
        return pair * 2 + 1 - pair % 2

    def far_outer(k):
        pair = at_z(k) // 2
        return pair * 2 + pair % 2

    def span(t, zz):
        return pl.ds(pl.multiple_of(t * TILE + zz * band2, 8), band2)

    def piece(t, zz, h):
        rows = band2 // BITS
        return pl.ds(pl.multiple_of(t * TILE + zz * band2 + h * rows, 8), rows)

    loads = {}
    for i, (name, src, dst) in enumerate((
            ("f1", f1_in, f1), ("f2", f2_in, f2.at[span(blk, z), :]), ("c3", c3_in, c3t),
            ("c2", c2_in, c2), ("c1", c1_in, c1), ("c0", c0_in, c0))):
        loads[name] = pltpu.make_async_copy(src, dst, in_sem.at[i])
        loads[name].start()

    peers = [{"rows": at_z(k)} for k in range(1, rows_n)]
    peers += [y_peer(k) for k in range(1, ys_n)]
    peers += [sib]
    barrier = pltpu.get_barrier_semaphore()
    for peer in peers:
        pl.semaphore_signal(barrier, inc=1, device_id=peer)
    table[...] = pool_table()
    loads["f1"].wait()
    high, low = split(f1[...])
    f1s[0:band, :] = high
    f1s[band:, :] = low
    turned = f1[...].T
    high, low = split(turned)
    f1t[:, 0:band] = high
    f1t[:, band:] = low
    loads["c3"].wait()
    loads["c2"].wait()
    loads["c1"].wait()
    c3 = c3t[...].T
    for t in range(tiles):
        coarse[t] = jnp.concatenate(
            [c1[:, t * POOL1:(t + 1) * POOL1], c2[:, t * POOL2:(t + 1) * POOL2],
             c3[:, t * POOL3:(t + 1) * POOL3],
             jnp.zeros((band, POOLED - POOL1 - POOL2 - POOL3), f32)], axis=1)
    loads["f2"].wait()
    pl.semaphore_wait(barrier, len(peers))

    sent = []

    def await_(ref, rsem):
        pltpu.make_async_copy(ref, ref, rsem).wait()

    def send(make):
        def copy():
            src, dst, ssem, rsem, peer = make()
            return pltpu.make_async_remote_copy(
                src_ref=src, dst_ref=dst, send_sem=ssem, recv_sem=rsem,
                device_id=peer, device_id_type=pl.DeviceIdType.MESH)

        copy().start()
        sent.append(copy)

    def whole_wait(t, zz):
        await_(f2.at[span(t, zz), :], ag_recv.at[t * rows_n + zz, 0])

    def piece_wait(t, zz, h):
        await_(f2.at[piece(t, zz, h), :], ag_recv.at[t * rows_n + zz, h])

    def whole(t, zz, ssem, peer, src=None):
        where = f2.at[span(t, zz), :]
        return where if src is None else src, where, ssem, ag_recv.at[t * rows_n + zz, 0], peer

    def cut(t, zz, h, ssem, peer, src=None):
        where = f2.at[piece(t, zz, h), :]
        return where if src is None else src, where, ssem, ag_recv.at[t * rows_n + zz, h], peer

    def to_sib(t, zz, src=None):
        send(lambda: whole(t(), zz(), cs_send.at[t() * rows_n + zz()], sib, src))

    def own_tile():
        return blk

    def y_tile(k):
        return lambda: at_y(k) * CORES + core

    def here():
        return z

    def beside():
        return partner

    ks = list(range(1, ys_n))
    ends = (far_inner, far_outer)
    for k in ks:
        send(lambda k=k: whole(blk, z, ys_send.at[k - 1, z, 0], y_peer(k)))
    for h in range(BITS):
        send(lambda h=h: cut(blk, z, h, own_send.at[0, h], {"rows": partner}))
    to_sib(own_tile, here)
    both = list(sent)
    sent.clear()

    @pl.when(inner)
    def _():
        for h in range(BITS):
            for j in pairs:
                send(lambda j=j, h=h: cut(blk, z, h, own_send.at[j // 2, h],
                                          {"rows": far_inner(j)}))

    only_inner = list(sent)
    sent.clear()

    loads["c0"].wait()

    def band_sum(t):
        high, low = split(coarse[t])
        spread = mm(jnp.concatenate([high, low], axis=0), table[...], 1, 1)
        total = c0[:, pl.ds(pl.multiple_of(t * TILE, TILE), TILE)] + (spread[:band] + spread[band:])
        high, low = split(total * inv_root)
        scaled[t, 0:band, :] = high
        scaled[t, band:, :] = low
        twice = jnp.concatenate([high, high], axis=0)
        value = mm(f1t[...], twice, 1, 0) + mm(f1t[:, 0:band], low, 1, 0)
        acc[t] = value.reshape(acc.shape[1:])

    def to_chip(k):
        yy = at_y(k)
        band_sum(yy * CORES + other)
        send(lambda: (acc.at[at_y(k) * CORES + other], cin.at[at_y(k)], rc_send.at[at_y(k)],
                      rc_recv.at[at_y(k)], sib))

    def chip_sum(k):
        yy = at_y(k)
        await_(cin.at[yy], rc_recv.at[yy])
        acc[yy * CORES + core] += cin[yy]

    def sums_to_y(k, zz, hs=range(CUTS)):
        for h in hs:
            send(lambda h=h: (
                acc.at[y_tile(k)(), zz(), h], yin.at[k - 1, zz(), h],
                ry_send.at[k - 1, zz(), h], ry_recv.at[k - 1, zz(), h], y_peer(k)))

    def add_y(zz, h):
        for k in ks:
            await_(yin.at[k - 1, zz, h], ry_recv.at[k - 1, zz, h])
            acc[blk, zz, h] += yin[k - 1, zz, h]

    def far(j, w):
        return lambda: ends[w](j)

    last = CUTS - 1

    for k in ks:
        to_chip(k)
    to_chip(0)
    for k in ks:
        band_sum(y_tile(k)())
        if k == ks[-1]:
            band_sum(blk)
        chip_sum(k)
        for j in pairs:
            sums_to_y(k, far(j, 1))
        for j in pairs:
            sums_to_y(k, far(j, 0), range(last))

    started = []

    def work(t):
        at = pl.ds(pl.multiple_of(t * TILE, TILE), TILE)
        high, low = split(f2[at, :])
        both = mm(f1s[...], high, 1, 1)
        value = (both[:band] + both[band:] + mm(f1s[0:band, :], low, 1, 1)) * inv_root
        o0[:, at] = value
        vh, vl = split(value)
        both = mm(jnp.concatenate([vh, vl], axis=0), table[...], 1, 0)
        both = both[:band] + both[band:]
        pooled[t] = both[:, POOL1:]
        o1[:, pl.ds(pl.multiple_of(t * POOL1, POOL1), POOL1)] = both[:, :POOL1]
        both = mm(scaled[t], high, 1, 0)
        grad = both[:band] + both[band:] + mm(scaled[t, 0:band, :], low, 1, 0)
        if started:
            gacc[...] += grad
        else:
            gacc[...] = grad
        started.append(t)

    def forward(j, w, h, peers, on):
        piece_wait(blk, ends[w](j), h)
        if on:
            send(lambda: cut(blk, ends[w](j), h, nf_send.at[j - 2 + w, h], {"rows": partner}))
        for k in peers:
            send(lambda k=k: cut(blk, ends[w](j), h, ys_send.at[k - 1, ends[w](j), h], y_peer(k)))
        if h == BITS - 1:
            to_sib(own_tile, far(j, w))

    def partner_piece(h, on):
        piece_wait(blk, partner, h)
        if on:
            for j in pairs:
                send(lambda j=j: cut(blk, partner, h, mf_send.at[0, j // 2 - 1, h],
                                     {"rows": far_inner(j)}))
        if h == BITS - 1:
            to_sib(own_tile, beside)

    def y_shard(k, on):
        whole_wait(y_tile(k)(), z)
        if on:
            for h in range(BITS):
                for j in pairs:
                    send(lambda j=j, h=h: cut(y_tile(k)(), z, h, mf_send.at[k, j // 2 - 1, h],
                                              {"rows": far_inner(j)}))
        to_sib(y_tile(k), here)

    def turn(k):
        send(lambda: whole(y_tile(k)(), z, zf_send.at[k - 1], {"rows": partner}))

    def sums(j, w, h, on):
        add_y(ends[w](j), h)
        if on:
            send(lambda: (acc.at[blk, ends[w](j), h], pin.at[j - 2 + w, h],
                          rp_send.at[j - 2 + w, h], rp_recv.at[j - 2 + w, h],
                          {"rows": partner}))

    def combine(j, w, h):
        await_(pin.at[j - 2 + w, h], rp_recv.at[j - 2 + w, h])
        acc[blk, ends[w](j), h] += pin[j - 2 + w, h]
        send(lambda: (acc.at[blk, ends[w](j), h],
                      xin.at[j // 2 - 1, h] if w else zin.at[j // 2, h],
                      rz_send.at[j - 1 + w, h],
                      rx_recv.at[j // 2 - 1, h] if w else rz_recv.at[j // 2, h],
                      {"rows": far_inner(j)}))

    def crossed(h):
        for j in pairs:
            await_(xin.at[j // 2 - 1, h], rx_recv.at[j // 2 - 1, h])
            acc[blk, partner, h] += xin[j // 2 - 1, h]

    def final(h, slots):
        add_y(z, h)
        total = acc[blk, z, h]
        for i in slots:
            await_(zin.at[i, h], rz_recv.at[i, h])
            total += zin[i, h]
            if i and h == last:
                await_(din.at[i - 1], rd_recv.at[i - 1])
                total += din[i - 1]
        some = chans // rows_n // CUTS
        g2_out[h * some:(h + 1) * some, :] = total

    def direct(j, is_inner):
        add_y(far_inner(j), last)
        send(lambda: (acc.at[blk, far_inner(j), last],
                      zin.at[j // 2, last] if is_inner else din.at[j // 2 - 1],
                      rz_send.at[j - 1, last],
                      rz_recv.at[j // 2, last] if is_inner else rd_recv.at[j // 2 - 1],
                      {"rows": far_inner(j)}))

    def partner_sums(h):
        send(lambda: (acc.at[blk, partner, h], zin.at[0, h], rz_send.at[0, h], rz_recv.at[0, h],
                      {"rows": partner}))

    def sib_wait():
        for zz in range(rows_n):
            whole_wait(y * CORES + other, zz)

    bits = [[(j, w, h) for j in pairs for h in range(BITS)] for w in range(2)]
    late = []
    both += sent
    sent.clear()
    mine = pl.ds(pl.multiple_of(z * band, band), band)

    def y_tiles(between):
        late.append(len(sent))
        for k in ks:
            t = y_tile(k)()
            whole_wait(t, partner)
            to_sib(y_tile(k), beside)
            for j in pairs:
                for w in range(2):
                    for h in range(BITS):
                        piece_wait(t, ends[w](j), h)
                    to_sib(y_tile(k), far(j, w))
            work(t)
        between()
        for k in ks:
            t = at_y(k) * CORES + other
            for zz in range(rows_n):
                whole_wait(t, zz)
            work(t)
        g1t[...] = gacc[...].T.reshape(rows_n, chans // rows_n, band)
        for k in range(rows_n - 1, 0, -1):
            send(lambda k=k: (g1t.at[at_z(k)], g1r.at[k - 1], g_send.at[k - 1],
                              g_recv.at[k - 1], {"rows": at_z(k)}))
        g1_out[:, mine] = g1t[z]

    halves = [(j, w, h) for j in pairs for w in range(2) for h in range(CUTS)]
    inners = [(j, w, h) for j, w, h in halves if w == 0 and h < last]
    outers = [(j, w, h) for j, w, h in halves if w == 1]

    def finish(slots, first):
        o2[...] = jnp.concatenate([pooled[t, :, :POOL2] for t in range(tiles)], axis=1)
        o3[...] = jnp.concatenate(
            [pooled[t, :, POOL2:POOL2 + POOL3] for t in range(tiles)], axis=1).T
        for copy in first + sent[:late[-1]]:
            copy().wait_send()
        for h in range(CUTS):
            final(h, slots)
        for k in range(1, rows_n):
            await_(g1r.at[k - 1], g_recv.at[k - 1])
            at = pl.multiple_of(at_z(k) * band, band)
            g1_out[:, pl.ds(at, band)] = g1r[k - 1]
        for copy in sent[late[-1]:]:
            copy().wait_send()


    @pl.when(inner)
    def _():
        for k in ks:
            sums_to_y(k, beside, range(last))
        partner_piece(0, True)
        for j, w, h in bits[0]:
            if h and j == 2:
                partner_piece(h, True)
            forward(j, w, h, [], True)
        for k in ks:
            y_shard(k, True)
        for j, w, h in bits[1]:
            forward(j, w, h, ks, True)
        for k in ks:
            turn(k)
            sums_to_y(k, beside, [last])
            for j in pairs:
                sums_to_y(k, far(j, 0), [last])
        for k in ks:
            for h in range(CUTS):
                await_(qin.at[k - 1, h], rq_recv.at[k - 1, h])
                acc[y_tile(k)(), z, h] += qin[k - 1, h]
            sums_to_y(k, here)
        chip_sum(0)
        for j, w, h in outers:
            sums(j, w, h, False)
        for j, w, h in inners:
            sums(j, w, h, False)
        work(blk)
        combine(*outers[0])
        sib_wait()
        work(y * CORES + other)
        for j, w, h in outers[1:]:
            combine(j, w, h)
        def rest(h):
            add_y(partner, h)
            crossed(h)
            partner_sums(h)

        y_tiles(lambda: [combine(*item) for item in inners])
        for h in range(CUTS):
            rest(h)
        for j in pairs:
            direct(j, True)
        finish(range(rows_n // 2), both + only_inner)

    started.clear()
    sent.clear()

    @pl.when(outer)
    def _():
        for k in ks:
            for h in range(CUTS):
                send(lambda k=k, h=h: (
                    acc.at[y_tile(k)(), partner, h], qin.at[k - 1, h], rq_send.at[k - 1, h],
                    rq_recv.at[k - 1, h], {"rows": partner}))
        for h in range(BITS):
            partner_piece(h, False)
        for k in ks:
            y_shard(k, False)
            turn(k)
        chip_sum(0)
        step = BITS // CUTS
        for w in (1, 0):
            for h in range(CUTS):
                for j in pairs:
                    if w or h < last:
                        sums(j, w, h, True)
                for j in pairs:
                    for b in range(h * step, h * step + step):
                        forward(j, 1 - w, b, ks, False)
        for k in ks:
            for j in pairs:
                sums_to_y(k, far(j, 0), [last])
            sums_to_y(k, here)
        for h in range(CUTS):
            partner_sums(h)
        work(blk)
        y_tiles(lambda: [direct(j, False) for j in pairs] + [sib_wait(), work(y * CORES + other)])
        finish([0], both)


def store(*refs):
    sems = refs[12]
    copies = [pltpu.make_async_copy(refs[i], refs[6 + i], sems.at[i]) for i in range(6)]
    for copy in copies:
        copy.start()
    for copy in copies:
        copy.wait()


def on_device(tiles, rows_n, frame_one, frame_two, cot_zero, cot_one, cot_two, cot_three):
    band, chans = frame_one.shape
    ys_n = tiles // CORES
    part = chans // rows_n
    some = part // CUTS
    cots = (cot_zero, cot_one, cot_two, cot_three)
    hbm = pl.BlockSpec(memory_space=pl.ANY)
    vmem = pl.BlockSpec(memory_space=pltpu.VMEM)
    dma = pltpu.SemaphoreType.DMA
    shapes = tuple(cot.shape for cot in cots[:3]) + (
        cot_three.shape[::-1], (part, band * rows_n), (part, TILE))
    made = pl.pallas_call(
        functools.partial(kernel, tiles, rows_n),
        out_shape=tuple(pltpu.VMEM(shape, f32) for shape in shapes),
        in_specs=[pl.BlockSpec(memory_space=pltpu.HBM)] * 6,
        out_specs=(vmem,) * 6,
        scratch_shapes=[
            pltpu.VMEM((band, chans), f32),
            pltpu.VMEM((tiles * TILE, chans), f32),
            pltpu.VMEM(cot_zero.shape, f32),
            pltpu.VMEM(cot_one.shape, f32),
            pltpu.VMEM(cot_two.shape, f32),
            pltpu.VMEM(cot_three.shape[::-1], f32),
            pltpu.VMEM((tiles, band, POOLED), f32),
            pltpu.VMEM((tiles, 2 * band, TILE), bf16),
            pltpu.VMEM((TILE, POOLED), bf16),
            pltpu.VMEM((2 * band, chans), bf16),
            pltpu.VMEM((chans, 2 * band), bf16),
            pltpu.VMEM((tiles, rows_n, CUTS, some, TILE), f32),
            pltpu.VMEM((ys_n, rows_n, CUTS, some, TILE), f32),
            pltpu.VMEM((ys_n - 1, rows_n, CUTS, some, TILE), f32),
            pltpu.VMEM((rows_n - 2, CUTS, some, TILE), f32),
            pltpu.VMEM((ys_n - 1, CUTS, some, TILE), f32),
            pltpu.VMEM((rows_n // 2 - 1, CUTS, some, TILE), f32),
            pltpu.VMEM((rows_n // 2 - 1, some, TILE), f32),
            pltpu.VMEM((rows_n // 2, CUTS, some, TILE), f32),
            pltpu.VMEM((tiles, band, POOLED - POOL1), f32),
            pltpu.VMEM((band, chans), f32),
            pltpu.VMEM((rows_n, part, band), f32),
            pltpu.VMEM((rows_n - 1, part, band), f32),
            dma((6,)),
            dma((tiles * rows_n, BITS)),
            dma((rows_n // 2, BITS)),
            dma((ys_n - 1, rows_n, BITS)),
            dma((tiles * rows_n,)),
            dma((ys_n - 1,)),
            dma((rows_n - 2, BITS)),
            dma((ys_n, rows_n // 2 - 1, BITS)),
            dma((ys_n,)), dma((ys_n,)),
            dma((ys_n - 1, rows_n, CUTS)), dma((ys_n - 1, rows_n, CUTS)),
            dma((rows_n - 2, CUTS)), dma((rows_n - 2, CUTS)),
            dma((ys_n - 1, CUTS)), dma((ys_n - 1, CUTS)),
            dma((rows_n - 1, CUTS)), dma((rows_n // 2, CUTS)), dma((rows_n // 2 - 1, CUTS)),
            dma((rows_n // 2 - 1,)),
            dma((rows_n - 1,)), dma((rows_n - 1,)),
        ],
        compiler_params=pltpu.CompilerParams(
            collective_id=0, has_side_effects=True, vmem_limit_bytes=48 << 20),
    )(*[pltpu.with_memory_space_constraint(value, pltpu.HBM) for value in (
        frame_one, frame_two, cot_zero, cot_one, cot_two, cot_three.T)])
    placed = pl.pallas_call(
        store,
        out_shape=tuple(jax.ShapeDtypeStruct(shape, f32) for shape in shapes),
        in_specs=[hbm] * 6,
        out_specs=(hbm,) * 6,
        scratch_shapes=[dma((6,))],
        compiler_params=pltpu.CompilerParams(vmem_limit_bytes=1 << 20),
    )(*[pltpu.with_memory_space_constraint(value, pltpu.VMEM) for value in made])
    return placed[:3] + (placed[3].T,) + placed[4:]


def solution(mesh):
    band = P(("groups", "blk", "rows"), None)
    turned = P("rows", ("groups", "blk"))
    return jax.shard_map(
        functools.partial(on_device, mesh.shape["blk"], mesh.shape["rows"]),
        mesh=mesh,
        in_specs=(band,) * 6,
        out_specs=(band,) * 4 + (turned,) * 2,
        check_vma=False,
    )
```
